32 devices in a mesh: groups: 2 (over y), seq: 8 (over z, x), head: 1, sub: 2 (over core).
Axes of the slice: x: 2, y: 2, z: 4, core: 2. Of those that a mesh axis runs over, the one named last changes fastest.
Arguments:
- ssm_input: bfloat16 [2048, 16384], P(('groups', 'seq'), ('head', 'sub')), parts along dimension 0, may hold values from -6 to 6
- gate_input: bfloat16 [2048, 16384], P(('groups', 'seq'), ('head', 'sub')), parts along dimension 0, may hold values from -6 to 6
- step: float32 [2048, 256], P(('groups', 'seq'), ('head', 'sub')), parts along dimension 0, may hold values from 0.5 to 2
- log_decay: float32 [2048, 256], P(('groups', 'seq'), ('head', 'sub')), parts along dimension 0, may hold values from -0.75 to 0
- b_input: bfloat16 [2048, 2048], P(('groups', 'seq'), 'head'), parts along dimension 0, may hold values from -6 to 6
- c_input: bfloat16 [2048, 2048], P(('groups', 'seq'), 'head'), parts along dimension 0, may hold values from -0.01171875 to 0.01171875
- d_skip: float32 [256], P(('head', 'sub')), may hold values from 0.5 to 2
- norm_gain: float32 [16384], P(('head', 'sub')), may hold values from 0.1 to 1.9
- queries: bfloat16 [2048, 8192], P(('groups', 'seq'), ('head', 'sub')), parts along dimension 0, may hold values from -120 to 120
- keys: bfloat16 [2048, 1024], P(('groups', 'seq'), 'head'), parts along dimension 0, may hold values from -5 to 5
- values: bfloat16 [2048, 1024], P(('groups', 'seq'), 'head'), parts along dimension 0, may hold values from -6 to 6
- segment_order: int32 [32], P('groups'), parts along dimension 0, may hold values from 0 to 15, each once
Outputs:
- mixer_out: bfloat16 [2048, 16384], P(('groups', 'seq'), ('head', 'sub')), parts along dimension 0
- attn_out: bfloat16 [2048, 8192], P(('groups', 'seq'), ('head', 'sub')), parts along dimension 0
The draws below stay inside these ranges and needn't reach their ends.
There are 2 independent parts, one for each index of `groups`. The reference program is written for one: setup_inputs(seed, part) draws one part's arguments, and reference() takes and returns one part's arrays. A program takes and returns all parts, laid end to end along the dimension named above; an argument that names none is the same for every part. Nothing has to cross between parts.
Inputs may be any that keep to these rules, and one draw needn't show every extreme that they name: `segment_order`: each number from 0 to 15 appears once.
All inputs are finite; a program needn't handle non-finite values.
Results may differ from the reference program's by a relative error of at most 0.009.
Values may be sent and summed in bfloat16 or wider, within the bound.
No kernel may reach another device: no remote copies, remote signals or barrier semaphores. Data moves between devices by JAX's collectives and lax.ppermute only.
A program may use at most 192 MiB of HBM per device.

```python
import math
import jax
import jax.numpy as jnp
from jax import lax

TOK_DEV = 128
SCAN_BLOCK = 128
MIXER_HEADS = 256
HEAD_DIM = 64
STATE = 256
GROUPS_BC = 8
ATT_HEADS = 64
KV_HEADS = 8
ATT_DIM = 128
PROMPT_TOKENS = 1024
SEGMENTS = 16
SEG_LEN = 64


def draw_log_decay(key, part):
    parallel_lanes = jax.random.split(key, 8)
    fast_share = 50
    fast_heads = jax.random.randint(parallel_lanes[0], (MIXER_HEADS,), 0, 100) < fast_share
    fast_rate = jnp.exp(jax.random.uniform(parallel_lanes[1], (MIXER_HEADS,), jnp.float32, math.log(1.0 / 50.0), math.log(1.0 / 25.0)))
    slow_rate = jnp.exp(jax.random.uniform(parallel_lanes[2], (MIXER_HEADS,), jnp.float32, math.log(0.05), math.log(0.25))) / PROMPT_TOKENS
    decay_rates = jnp.where(fast_heads, fast_rate, slow_rate)
    split_multiplier = jnp.exp(jax.random.uniform(parallel_lanes[3], (PROMPT_TOKENS // TOK_DEV, 1, MIXER_HEADS), jnp.float32, math.log(0.5), math.log(2.0)))
    split_multiplier = jnp.broadcast_to(split_multiplier, (PROMPT_TOKENS // TOK_DEV, TOK_DEV, MIXER_HEADS)).reshape(PROMPT_TOKENS, MIXER_HEADS)
    noise_level = jax.random.uniform(parallel_lanes[4], (PROMPT_TOKENS, MIXER_HEADS), jnp.float32, 0.5, 1.5)
    leading_group = jax.random.randint(parallel_lanes[5], (MIXER_HEADS,), 0, PROMPT_TOKENS)
    trailing_group = jax.random.randint(parallel_lanes[6], (MIXER_HEADS,), 0, PROMPT_TOKENS)
    device_slots = jnp.arange(PROMPT_TOKENS, dtype=jnp.int32)[:, None]
    mixing_amplitude = jax.random.uniform(parallel_lanes[7], (PROMPT_TOKENS, MIXER_HEADS), jnp.float32, 0.22, 0.6)
    token_groups = jnp.where((device_slots == leading_group[None, :]) | (device_slots == trailing_group[None, :]), mixing_amplitude, 0.0)
    return -(decay_rates[None, :] * split_multiplier * noise_level + token_groups)


def query_key_base(key):
    base_key = jax.random.fold_in(key, 11)
    parallel_lanes = jax.random.split(base_key, 1)
    key_values = jnp.clip(jax.random.normal(parallel_lanes[0], (PROMPT_TOKENS, KV_HEADS, ATT_DIM), jnp.float32), -5.0, 5.0)
    return key_values


def draw_keys(key, part):
    key_values = query_key_base(key)
    return key_values.reshape(PROMPT_TOKENS, KV_HEADS * ATT_DIM).astype(jnp.bfloat16)


def draw_queries(key, part):
    own = jnp.clip(jax.random.normal(jax.random.fold_in(key, 12), (PROMPT_TOKENS, ATT_HEADS, ATT_DIM), jnp.float32), -5.0, 5.0)
    return own.reshape(PROMPT_TOKENS, ATT_HEADS * ATT_DIM).astype(jnp.bfloat16)


def steps_of(key, extent, cuts, least, top_value):
    loudness, own = 1.0, jax.random.fold_in(key, 6)
    for position, shards_of in cuts:
        draws = jnp.exp(jax.random.uniform(jax.random.fold_in(own, position), (shards_of,), jnp.float32, least / len(cuts), top_value / len(cuts)))
        loudness = loudness * jnp.repeat(draws, extent[position] // shards_of).reshape([-1 if axis == position else 1 for axis in range(len(extent))])
    return loudness


def scatter_about(key, shape, scale, limit, cuts=(), held_as=jnp.bfloat16):
    values = scale * jax.random.normal(key, shape, jnp.float32)
    if cuts:
        values = values * steps_of(key, shape, cuts, -0.22, 0.18)
    return jnp.clip(values, -limit, limit).astype(held_as)


def setup_inputs(seed: int = 0, part: int = 0) -> dict:
    splits = jax.random.split(jax.random.key(seed), 13)
    part_splits = jax.random.split(jax.random.fold_in(splits[12], part), 13)
    ssm_input = scatter_about(part_splits[0], (PROMPT_TOKENS, MIXER_HEADS * HEAD_DIM), 1.0, 6.0, ((0, 8), (1, 2)))
    gate_input = scatter_about(part_splits[1], (PROMPT_TOKENS, MIXER_HEADS * HEAD_DIM), 1.0, 6.0, ((0, 8), (1, 2)))
    step = jnp.clip(jnp.exp(math.log(2.0) - 1.3862944 * jax.random.uniform(part_splits[2], (PROMPT_TOKENS, MIXER_HEADS), jnp.float32) ** steps_of(part_splits[2], (PROMPT_TOKENS, MIXER_HEADS), ((0, 8), (1, 2)), -0.2, 0.2)), 0.5, 2.0)
    log_decay = draw_log_decay(jax.random.fold_in(jax.random.fold_in(splits[12], part), 71), part)
    b_input = scatter_about(part_splits[4], (PROMPT_TOKENS, GROUPS_BC * STATE), 1.0, 6.0, ((0, 8),))
    c_input = scatter_about(part_splits[5], (PROMPT_TOKENS, GROUPS_BC * STATE), ((STATE * PROMPT_TOKENS) ** -0.5), 0.01171875, ((0, 8),))
    d_skip = jnp.clip(jnp.exp(math.log(2.0) - 1.3862944 * jax.random.uniform(splits[6], (MIXER_HEADS,), jnp.float32) ** steps_of(splits[6], (MIXER_HEADS,), ((0, 2),), -0.2, 0.2)), 0.5, 2.0)
    norm_gain = jnp.clip(1.0 + 0.18 * jax.random.normal(splits[7], (MIXER_HEADS * HEAD_DIM,), jnp.float32), 0.1, 1.9)
    queries = draw_queries(jax.random.fold_in(jax.random.fold_in(splits[12], part), 71), part)
    keys = draw_keys(jax.random.fold_in(jax.random.fold_in(splits[12], part), 71), part)
    values = scatter_about(part_splits[10], (PROMPT_TOKENS, KV_HEADS * ATT_DIM), 1.0, 6.0, ((0, 8),))
    segment_order = jax.random.permutation(part_splits[11], SEGMENTS).astype(jnp.int32)
    return {"ssm_input": ssm_input, "gate_input": gate_input, "step": step, "log_decay": log_decay, "b_input": b_input, "c_input": c_input, "d_skip": d_skip, "norm_gain": norm_gain, "queries": queries, "keys": keys, "values": values, "segment_order": segment_order}


def rounded(value):
    return lax.optimization_barrier(value.astype(jnp.bfloat16)).astype(jnp.float32)

def ssm_group(operands):
    inputs, gates, steps, decays, b_rows, c_rows, skips, gains = operands
    cumulated = jnp.cumsum(decays, axis=1)
    scaled = rounded(inputs.astype(jnp.float32) * steps[..., None])
    intersections = jnp.einsum('cqn,ckn->cqk', c_rows.astype(jnp.float32), b_rows.astype(jnp.float32))
    gaps = cumulated[:, :, None, :] - cumulated[:, None, :, :]
    lower = jnp.tril(jnp.ones((SCAN_BLOCK, SCAN_BLOCK), dtype=bool))
    weights = rounded(jnp.where(lower[None, :, :, None], jnp.exp(gaps), 0.0) * intersections[..., None])
    within = jnp.einsum('cqkh,ckhp->cqhp', weights, scaled)
    ends = cumulated[:, -1, :]
    weighted_b = rounded(jnp.exp(ends[:, None, :] - cumulated)[..., None] * b_rows.astype(jnp.float32)[:, :, None, :])
    contributions = jnp.einsum('ckhn,ckhp->chnp', weighted_b, scaled)
    factors = jnp.exp(ends)

    def advance(state, pair):
        factor, contribution = pair
        return (factor[:, None, None] * state + contribution, state)
    start_state = jnp.zeros(contributions.shape[1:], jnp.float32)
    final_state, entering = lax.scan(advance, start_state, (factors, contributions))
    carried = jnp.einsum('cqn,chnp->cqhp', c_rows.astype(jnp.float32), rounded(entering)) * jnp.exp(cumulated)[..., None]
    mixed = within + carried + skips[None, None, :, None] * inputs.astype(jnp.float32)
    gated = mixed * jax.nn.silu(gates.astype(jnp.float32))
    mean_square = lax.optimization_barrier(jnp.mean(gated * gated, axis=3))
    normed = gated * lax.rsqrt(mean_square + 1e-05)[..., None] * gains[None, None]
    return normed.astype(jnp.bfloat16)

def reference(ssm_input, gate_input, step, log_decay, b_input, c_input, d_skip, norm_gain, queries, keys, values, segment_order):
    per_group = MIXER_HEADS // GROUPS_BC
    blocks = PROMPT_TOKENS // SCAN_BLOCK
    inputs = ssm_input.reshape(blocks, SCAN_BLOCK, GROUPS_BC, per_group, HEAD_DIM).transpose(2, 0, 1, 3, 4)
    gates = gate_input.reshape(blocks, SCAN_BLOCK, GROUPS_BC, per_group, HEAD_DIM).transpose(2, 0, 1, 3, 4)
    steps = step.reshape(blocks, SCAN_BLOCK, GROUPS_BC, per_group).transpose(2, 0, 1, 3)
    decays = log_decay.reshape(blocks, SCAN_BLOCK, GROUPS_BC, per_group).transpose(2, 0, 1, 3)
    b_rows = b_input.reshape(blocks, SCAN_BLOCK, GROUPS_BC, STATE).transpose(2, 0, 1, 3)
    c_rows = c_input.reshape(blocks, SCAN_BLOCK, GROUPS_BC, STATE).transpose(2, 0, 1, 3)
    skips = d_skip.reshape(GROUPS_BC, per_group)
    gains = norm_gain.reshape(GROUPS_BC, per_group, HEAD_DIM)
    mixed = lax.map(ssm_group, (inputs, gates, steps, decays, b_rows, c_rows, skips, gains))
    mixer_out = mixed.transpose(1, 2, 0, 3, 4).reshape(PROMPT_TOKENS, MIXER_HEADS * HEAD_DIM)
    ratio = ATT_HEADS // KV_HEADS
    positions = (segment_order[:, None] * SEG_LEN + jnp.arange(SEG_LEN, dtype=jnp.int32)[None, :]).reshape(PROMPT_TOKENS)
    query_groups = queries.reshape(PROMPT_TOKENS // TOK_DEV, TOK_DEV, KV_HEADS, ratio, ATT_DIM)
    query_positions = positions.reshape(PROMPT_TOKENS // TOK_DEV, TOK_DEV)
    key_heads = keys.reshape(PROMPT_TOKENS, KV_HEADS, ATT_DIM).astype(jnp.float32)
    value_heads = values.reshape(PROMPT_TOKENS, KV_HEADS, ATT_DIM).astype(jnp.float32)

    def attend_block(operands):
        block_queries, block_positions = operands
        scores = jnp.einsum('tgrd,sgd->tgrs', block_queries.astype(jnp.float32), key_heads) * ATT_DIM ** (-0.5)
        visible = positions[None, :] <= block_positions[:, None]
        scores = jnp.where(visible[:, None, None, :], scores, -jnp.inf)
        peak = lax.optimization_barrier(jnp.max(scores, axis=-1, keepdims=True))
        expos = jnp.exp(scores - peak)
        totals = lax.optimization_barrier(jnp.sum(expos, axis=-1))
        summed = jnp.einsum('tgrs,sgd->tgrd', rounded(expos), value_heads)
        return (summed / totals[..., None]).astype(jnp.bfloat16)
    attended = lax.map(attend_block, (query_groups, query_positions))
    attn_out = attended.reshape(PROMPT_TOKENS, ATT_HEADS * ATT_DIM)
    return (mixer_out, attn_out)
```

```python
import functools
import math
import jax
import jax.numpy as jnp
from jax import lax
from jax.experimental import pallas as pl
from jax.experimental.pallas import tpu as pltpu
from jax.sharding import PartitionSpec as P

SCAN_BLOCK = 128
MIXER_HEADS = 256
STATE = 256
GROUPS_BC = 8
ATT_HEADS = 64
KV_HEADS = 8
ATT_DIM = 128
WIDTH = 64
PER_GROUP = MIXER_HEADS // GROUPS_BC
CHUNKS = 4
F32 = jnp.float32
BF16 = jnp.bfloat16


def dot(a, b, dims=((1,), (0,))):
    return lax.dot_general(a, b, (dims, ((), ())), preferred_element_type=F32)


def pair_columns(cols, j):
    lane = lax.broadcasted_iota(jnp.int32, (cols.shape[0], 2 * WIDTH), 1)
    return jnp.where(lane < WIDTH, cols[:, 2 * j : 2 * j + 1], cols[:, 2 * j + 1 : 2 * j + 2])


def expand(cols):
    return jnp.concatenate([pair_columns(cols, j) for j in range(cols.shape[1] // 2)], axis=1)


def call(body, grid, in_specs, out_specs, out_shape, scratch=(), aliases={}):
    return pl.pallas_call(
        body,
        out_shape=out_shape,
        grid_spec=pltpu.PrefetchScalarGridSpec(
            num_scalar_prefetch=1,
            grid=grid,
            in_specs=in_specs,
            out_specs=out_specs,
            scratch_shapes=list(scratch),
        ),
        input_output_aliases=aliases,
    )


def shaped(shape, dtype):
    return jax.ShapeDtypeStruct(shape, dtype)


def whole(shape):
    zeros = (0,) * len(shape)
    return pl.BlockSpec(shape, lambda *_: zeros)


def scalars_body(_, step_ref, decay_ref, stepb, cumb, wb, endb, cumt):
    rows, heads = step_ref.shape
    chunks, width = stepb.shape[0], stepb.shape[2]
    decay = decay_ref[...]
    lower = (
        lax.broadcasted_iota(jnp.int32, (rows, rows), 0)
        >= lax.broadcasted_iota(jnp.int32, (rows, rows), 1)
    ).astype(F32)
    cum = lax.dot_general(
        lower, decay, (((1,), (0,)), ((), ())), precision=lax.Precision.HIGHEST,
        preferred_element_type=F32,
    )
    end = cum[rows - 1 : rows, :]
    w = jnp.exp(end - cum)
    factor = jnp.exp(end)
    cumt[...] = cum.T
    for j in range(chunks):
        cut = slice(j * width, (j + 1) * width)
        stepb[j] = step_ref[:, cut]
        cumb[j] = cum[:, cut]
        wb[j] = w[:, cut]
        endb[j] = factor[:, cut]


def weighted_inputs(x, step, w):
    parts = []
    for j in range(step.shape[1] // 2):
        cut = slice(j * 2 * WIDTH, (j + 1) * 2 * WIDTH)
        scaled = (x[:, cut].astype(F32) * pair_columns(step, j)).astype(BF16)
        parts.append((scaled.astype(F32) * pair_columns(w, j)).astype(BF16))
    return jnp.concatenate(parts, axis=1)


def send_body(_, x_ref, step_ref, w_ref, out_ref):
    out_ref[...] = weighted_inputs(x_ref[...], step_ref[0], w_ref[0])


def plane_body(
    meta, x_ref, step_ref, w_ref, end_ref, b_own, c_own, sd_oth, b_oth, c_oth, end_oth,
    total_ref, send_ref, inner_ref,
):
    first = meta[0] == 0
    own = dot(b_own[...], weighted_inputs(x_ref[...], step_ref[0], w_ref[0]), ((0,), (0,)))
    oth = dot(b_oth[...], sd_oth[...], ((0,), (0,)))
    d_own, d_oth = expand(end_ref[0]), expand(end_oth[0])
    one = jnp.ones_like(d_own)
    total = own * jnp.where(first, d_oth, one) + oth * jnp.where(first, one, d_own)
    total_ref[...] = total
    send_ref[...] = total.astype(BF16)
    earlier = jnp.where(first, own, oth).astype(BF16)
    c_later = jnp.where(first, c_oth[...].astype(F32), c_own[...].astype(F32)).astype(BF16)
    inner_ref[...] = dot(c_later, earlier)


def hop_body(_, recv_ref, total_ref, end_ref, end_oth, out_ref):
    d = expand(end_ref[0] * end_oth[0])
    out_ref[...] = (d * recv_ref[...].astype(F32) + total_ref[...]).astype(BF16)


def carried_body(hops, meta, *refs):
    recvs = refs[:hops]
    c_own, c_oth, inner_ref, end_ref, end_oth, own_ref, oth_ref = refs[hops:]
    first = meta[0] == 0
    state = recvs[0][...].astype(F32)
    for r in recvs[1:]:
        state = state + r[...].astype(F32)
    state = state.astype(BF16)
    d_own, d_oth = expand(end_ref[0]), expand(end_oth[0])
    one = jnp.ones_like(d_own)
    inner = inner_ref[...]
    zero = jnp.zeros_like(inner)
    own = dot(c_own[...], state) * jnp.where(first, one, d_oth) + jnp.where(first, zero, inner)
    oth = dot(c_oth[...], state) * jnp.where(first, d_own, one) + jnp.where(first, inner, zero)
    own_ref[...] = own.astype(BF16)
    oth_ref[...] = oth.astype(BF16)


def within_body(_, x_ref, step_ref, cum_ref, cumt_ref, skip_ref, b_ref, c_ref, out_ref):
    rows = x_ref.shape[0]
    above = lax.broadcasted_iota(jnp.int32, (rows, rows), 0) < lax.broadcasted_iota(
        jnp.int32, (rows, rows), 1
    )
    inter = jnp.where(above, 0.0, dot(c_ref[...], b_ref[...], ((1,), (1,))))
    lane = lax.broadcasted_iota(jnp.int32, (rows, 2 * WIDTH), 1)
    step, cum, skip = step_ref[0], cum_ref[0], skip_ref[0]
    for j in range(step.shape[1] // 2):
        cut = slice(j * 2 * WIDTH, (j + 1) * 2 * WIDTH)
        x = x_ref[:, cut].astype(F32)
        scaled = x * pair_columns(step, j)
        weights = []
        for h in (2 * j, 2 * j + 1):
            gap = jnp.minimum(cum[:, h : h + 1] - cumt_ref[0, h : h + 1, :], 0.0)
            weights.append((jnp.exp(gap) * inter).astype(BF16))
        stacked = jnp.concatenate(
            [
                jnp.where(lane < WIDTH, scaled, 0.0).astype(BF16),
                jnp.where(lane < WIDTH, 0.0, scaled).astype(BF16),
            ],
            axis=0,
        )
        out_ref[:, cut] = dot(jnp.concatenate(weights, axis=1), stacked) + x * pair_columns(skip, j)


def gate_body(meta, mixed_ref, carried_ref, gate_ref, cum_ref, gain_ref, *rest):
    out_ref = rest[-1]
    cum = jnp.exp(cum_ref[0])
    size = 2 * WIDTH
    same = (
        lax.broadcasted_iota(jnp.int32, (size, size), 0) // WIDTH
        == lax.broadcasted_iota(jnp.int32, (size, size), 1) // WIDTH
    )
    mean = jnp.where(same, 1.0 / WIDTH, 0.0).astype(BF16)
    for j in range(cum.shape[1] // 2):
        cut = slice(j * size, (j + 1) * size)
        mixed = mixed_ref[:, cut] + carried_ref[:, cut].astype(F32) * pair_columns(cum, j)
        gate = gate_ref[:, cut].astype(F32)
        gated = mixed * (gate / (1.0 + jnp.exp(-gate)))
        square = gated * gated
        high = square.astype(BF16)
        low = (square - high.astype(F32)).astype(BF16)
        mean_square = dot(high, mean) + dot(low, mean)
        out_ref[:, cut] = (gated * lax.rsqrt(mean_square + 1e-05) * gain_ref[:, cut]).astype(BF16)


def attend_body(per_used, _, q_ref, *refs):
    keys, values = refs[0:2], refs[2:4]
    qpos_ref, kpos_ref, out_ref, bias = refs[4:]

    @pl.when(pl.program_id(0) == 0)
    def _():
        bias[...] = jnp.where(kpos_ref[...] <= qpos_ref[...], 0.0, -jnp.inf)

    shape = (-1, ATT_DIM)
    key = jnp.concatenate([k[...].reshape(shape) for k in keys], axis=0)
    value = jnp.concatenate([v[...].reshape(shape) for v in values], axis=0)
    factor = ATT_DIM ** (-0.5) * math.log2(math.e)
    for r in range(per_used):
        cut = slice(r * ATT_DIM, (r + 1) * ATT_DIM)
        scores = dot(q_ref[:, cut], key, ((1,), (1,))) + bias[...]
        peak = jnp.max(scores, axis=1, keepdims=True)
        expos = jnp.exp2((scores - peak) * factor)
        total = jnp.sum(expos, axis=1, keepdims=True)
        out_ref[:, cut] = (dot(expos.astype(BF16), value) / total).astype(BF16)


def local(
    ssm_input, gate_input, step, log_decay, b_input, c_input, d_skip, norm_gain,
    queries, keys, values, segment_order,
):
    rows, heads = step.shape
    peers, here = lax.axis_size("seq"), lax.axis_index("seq")
    sub_index = lax.axis_index("sub")
    planes = peers // 2
    side, plane = here % 2, here // 2
    half = heads // 2
    count = CHUNKS
    per_chunk = half // count
    wide = per_chunk * WIDTH
    chunks = 2 * count
    swap = [(i, i ^ 1) for i in range(peers)]
    up = [(i, i + 2) for i in range(peers - 2)]
    down = [(i + 2, i) for i in range(peers - 2)]

    query_count = queries.shape[1] // ATT_DIM
    ratio = ATT_HEADS // KV_HEADS
    used_heads = max(1, query_count // ratio)
    per_used = query_count // used_heads
    first_head = sub_index * query_count // ratio
    kv_wide = used_heads * ATT_DIM
    start = first_head * ATT_DIM
    pack = jnp.concatenate(
        [
            lax.dynamic_slice_in_dim(keys, start, kv_wide, 1),
            lax.dynamic_slice_in_dim(values, start, kv_wide, 1),
        ],
        axis=1,
    )
    gathered = jnp.zeros((planes + 1,) + pack.shape, BF16)
    gathered = lax.dynamic_update_slice_in_dim(gathered, pack[None], plane, 0)
    rising = falling = pack
    for i in range(1, planes):
        rising = lax.ppermute(rising, "seq", up)
        falling = lax.ppermute(falling, "seq", down)
        gathered = lax.dynamic_update_slice_in_dim(
            gathered, rising[None], jnp.where(plane >= i, plane - i, planes), 0
        )
        gathered = lax.dynamic_update_slice_in_dim(
            gathered, falling[None], jnp.where(plane + i < planes, plane + i, planes), 0
        )
    other_side = lax.ppermute(gathered[:planes], "seq", swap)

    stepb, cumb, wb, endb, cumt = call(
        scalars_body,
        (1,),
        [whole((rows, heads))] * 2,
        [whole((chunks, rows, per_chunk))] * 3 + [whole((chunks, 1, per_chunk)), whole((heads, rows))],
        [shaped((chunks, rows, per_chunk), F32)] * 3
        + [shaped((chunks, 1, per_chunk), F32), shaped((heads, rows), F32)],
    )(jnp.zeros((1,), jnp.int32), step, log_decay)

    base = sub_index * heads
    group_of = lambda chunk: (base + chunk * per_chunk) // PER_GROUP
    groups_half = max(1, half // PER_GROUP)
    given = (1 - side) * half
    bc_start = ((base + given) // PER_GROUP) * STATE
    bc_oth = lax.ppermute(
        jnp.concatenate(
            [
                lax.dynamic_slice_in_dim(b_input, bc_start, groups_half * STATE, 1),
                lax.dynamic_slice_in_dim(c_input, bc_start, groups_half * STATE, 1),
            ],
            axis=1,
        ),
        "seq",
        swap,
    )
    end_oth = lax.ppermute(
        lax.dynamic_slice_in_dim(endb, (1 - side) * count, count, 0), "seq", swap
    )

    narrow = lambda size=rows: pl.BlockSpec((1, size, per_chunk), lambda i, m: (m[1], 0, 0))
    columns = pl.BlockSpec((rows, wide), lambda i, m: (0, m[1]))
    sd_oth = []
    for c in range(count):
        meta = jnp.stack([side, (1 - side) * count + c])
        sd = call(
            send_body, (1,), [columns, narrow(), narrow()], whole((rows, wide)),
            shaped((rows, wide), BF16),
        )(meta, ssm_input, stepb, wb)
        sd_oth.append(lax.ppermute(sd, "seq", swap))

    group_block = pl.BlockSpec((rows, STATE), lambda i, m: (0, m[2]))
    metas, totals, sends, inners = [], [], [], []
    for c in range(count):
        mine = side * count + c
        meta = jnp.stack([side, mine, group_of(mine)])
        in_half = c * per_chunk // PER_GROUP
        oth_block = lambda at: pl.BlockSpec((rows, STATE), lambda i, m, at=at: (0, at))
        oth_end = pl.BlockSpec((1, 1, per_chunk), lambda i, m, c=c: (c, 0, 0))
        total, send, inner = call(
            plane_body,
            (1,),
            [
                columns, narrow(), narrow(), narrow(1), group_block, group_block,
                whole((rows, wide)), oth_block(in_half), oth_block(groups_half + in_half), oth_end,
            ],
            [whole((STATE, wide)), whole((STATE, wide)), whole((rows, wide))],
            [shaped((STATE, wide), F32), shaped((STATE, wide), BF16), shaped((rows, wide), F32)],
        )(meta, ssm_input, stepb, wb, endb, b_input, c_input, sd_oth[c], bc_oth, bc_oth, end_oth)
        metas.append((meta, in_half, oth_block, oth_end))
        totals.append(total)
        sends.append(send)
        inners.append(inner)

    received = [[] for _ in range(count)]
    for wave in range(count + planes - 2):
        for h in range(planes - 1):
            c = wave - h
            if not 0 <= c < count:
                continue
            meta, _, _, oth_end = metas[c]
            got = lax.ppermute(sends[c], "seq", [(2 * h + x, 2 * h + 2 + x) for x in range(2)])
            received[c].append(got)
            if h < planes - 2:
                sends[c] = call(
                    hop_body,
                    (1,),
                    [whole((STATE, wide)), whole((STATE, wide)), narrow(1), oth_end],
                    whole((STATE, wide)),
                    shaped((STATE, wide), BF16),
                )(meta, got, totals[c], endb, end_oth)

    skips = d_skip.reshape(chunks, 1, per_chunk)
    mixed = call(
        within_body,
        (chunks,),
        [
            pl.BlockSpec((rows, wide), lambda i, m: (0, i)),
            pl.BlockSpec((1, rows, per_chunk), lambda i, m: (i, 0, 0)),
            pl.BlockSpec((1, rows, per_chunk), lambda i, m: (i, 0, 0)),
            pl.BlockSpec((1, per_chunk, rows), lambda i, m: (i, 0, 0)),
            pl.BlockSpec((1, 1, per_chunk), lambda i, m: (i, 0, 0)),
            pl.BlockSpec((rows, STATE), lambda i, m: (0, m[i])),
            pl.BlockSpec((rows, STATE), lambda i, m: (0, m[i])),
        ],
        pl.BlockSpec((rows, wide), lambda i, m: (0, i)),
        shaped((rows, heads * WIDTH), F32),
    )(
        group_of(jnp.arange(chunks, dtype=jnp.int32)), ssm_input, stepb, cumb,
        cumt.reshape(chunks, per_chunk, rows), skips, b_input, c_input,
    )

    gains = norm_gain.reshape(1, heads * WIDTH)
    mixer_out = None

    def finish(mixer_out, chunk, carried):
        specs = [
            columns, whole((rows, wide)), columns, narrow(),
            pl.BlockSpec((1, wide), lambda i, m: (0, m[1])),
        ]
        args = [mixed, carried, gate_input, cumb, gains]
        aliases = {}
        if mixer_out is not None:
            specs.append(pl.BlockSpec(memory_space=pl.ANY))
            args.append(mixer_out)
            aliases = {len(args): 0}
        return call(
            gate_body, (1,), specs, columns, shaped((rows, heads * WIDTH), BF16), aliases=aliases
        )(jnp.stack([side, chunk]), *args)

    back = []
    for c in range(count):
        meta, in_half, oth_block, oth_end = metas[c]
        own, oth = call(
            functools.partial(carried_body, planes - 1),
            (1,),
            [whole((STATE, wide))] * (planes - 1)
            + [group_block, oth_block(groups_half + in_half), whole((rows, wide)), narrow(1), oth_end],
            [whole((rows, wide))] * 2,
            [shaped((rows, wide), BF16)] * 2,
        )(meta, *received[c], c_input, bc_oth, inners[c], endb, end_oth)
        back.append(lax.ppermute(oth, "seq", swap))
        mixer_out = finish(mixer_out, side * count + c, own)
    for c in range(count):
        mixer_out = finish(mixer_out, (1 - side) * count + c, back[c])

    seg_len = rows * peers // segment_order.shape[0]

    def positions(block):
        at = block[:, None] * rows + jnp.arange(rows, dtype=jnp.int32)[None, :]
        at = at.reshape(-1)
        return segment_order[at // seg_len] * seg_len + at % seg_len

    every = jnp.arange(planes, dtype=jnp.int32) * 2
    key_pos = positions(jnp.concatenate([every + side, every + 1 - side]))[None, :]
    query_pos = positions(here[None])[:, None]
    kv_spec = lambda at, lead: pl.BlockSpec(
        (planes, rows, ATT_DIM), lambda g, m, at=at: (0, 0, at + g)
    )
    attn_out = call(
        functools.partial(attend_body, per_used),
        (used_heads,),
        [pl.BlockSpec((rows, per_used * ATT_DIM), lambda g, m: (0, g))]
        + [kv_spec(0, 0), kv_spec(0, 0), kv_spec(used_heads, 0), kv_spec(used_heads, 0)]
        + [whole(query_pos.shape), whole(key_pos.shape)],
        pl.BlockSpec((rows, per_used * ATT_DIM), lambda g, m: (0, g)),
        shaped(queries.shape, BF16),
        scratch=[pltpu.VMEM((rows, key_pos.shape[1]), F32)],
    )(
        jnp.zeros((1,), jnp.int32), queries, gathered, other_side, gathered, other_side,
        query_pos, key_pos,
    )
    return mixer_out, attn_out


def solution(mesh):
    tokens = ("groups", "seq")
    both = ("head", "sub")
    placed = (
        P(tokens, both), P(tokens, both), P(tokens, both), P(tokens, both),
        P(tokens, "head"), P(tokens, "head"), P(both), P(both),
        P(tokens, both), P(tokens, "head"), P(tokens, "head"), P("groups"),
    )
    return jax.shard_map(
        local,
        mesh=mesh,
        in_specs=placed,
        out_specs=(P(tokens, both), P(tokens, both)),
        check_vma=False,
    )
```

```python
import functools
import math
import jax
import jax.numpy as jnp
from jax import lax
from jax.experimental import pallas as pl
from jax.experimental.pallas import tpu as pltpu
from jax.sharding import PartitionSpec as P

SCAN_BLOCK = 128
MIXER_HEADS = 256
STATE = 256
GROUPS_BC = 8
ATT_HEADS = 64
KV_HEADS = 8
ATT_DIM = 128
WIDTH = 64
PER_GROUP = MIXER_HEADS // GROUPS_BC
CHUNKS = 4
SENDS = 2
SIDE, OWN, GIVEN, PLANE, GROUP = range(5)
F32 = jnp.float32
BF16 = jnp.bfloat16


def dot(a, b, dims=((1,), (0,))):
    return lax.dot_general(a, b, (dims, ((), ())), preferred_element_type=F32)


def pair_columns(cols, j):
    lane = lax.broadcasted_iota(jnp.int32, (cols.shape[0], 2 * WIDTH), 1)
    return jnp.where(lane < WIDTH, cols[:, 2 * j : 2 * j + 1], cols[:, 2 * j + 1 : 2 * j + 2])


def expand(cols):
    return jnp.concatenate([pair_columns(cols, j) for j in range(cols.shape[1] // 2)], axis=1)


def call(body, grid, in_specs, out_specs, out_shape, scratch=(), aliases={}):
    return pl.pallas_call(
        body,
        out_shape=out_shape,
        grid_spec=pltpu.PrefetchScalarGridSpec(
            num_scalar_prefetch=1,
            grid=grid,
            in_specs=in_specs,
            out_specs=out_specs,
            scratch_shapes=list(scratch),
        ),
        input_output_aliases=aliases,
    )


def shaped(shape, dtype):
    return jax.ShapeDtypeStruct(shape, dtype)


def whole(shape):
    zeros = (0,) * len(shape)
    return pl.BlockSpec(shape, lambda *_: zeros)


def scalars_body(_, step_ref, decay_ref, stepb, cumb, wb, endb, cumt):
    rows, heads = step_ref.shape
    chunks, width = stepb.shape[0], stepb.shape[2]
    decay = decay_ref[...]
    lower = (
        lax.broadcasted_iota(jnp.int32, (rows, rows), 0)
        >= lax.broadcasted_iota(jnp.int32, (rows, rows), 1)
    ).astype(F32)
    cum = lax.dot_general(
        lower, decay, (((1,), (0,)), ((), ())), precision=lax.Precision.HIGHEST,
        preferred_element_type=F32,
    )
    end = cum[rows - 1 : rows, :]
    w = jnp.exp(end - cum)
    factor = jnp.exp(end)
    cumt[...] = cum.T
    for j in range(chunks):
        cut = slice(j * width, (j + 1) * width)
        stepb[j] = step_ref[:, cut]
        cumb[j] = cum[:, cut]
        wb[j] = w[:, cut]
        endb[j] = factor[:, cut]


def weighted_inputs(x, step, w):
    parts = []
    for j in range(step.shape[1] // 2):
        cut = slice(j * 2 * WIDTH, (j + 1) * 2 * WIDTH)
        scaled = (x[:, cut].astype(F32) * pair_columns(step, j)).astype(BF16)
        parts.append((scaled.astype(F32) * pair_columns(w, j)).astype(BF16))
    return jnp.concatenate(parts, axis=1)


def send_body(_, x_ref, step_ref, w_ref, out_ref):
    out_ref[0] = weighted_inputs(x_ref[...], step_ref[0], w_ref[0])


def plane_body(
    meta, x_ref, step_ref, w_ref, end_ref, b_own, c_own, sd_oth, b_oth, c_oth, end_oth,
    total_ref, inner_ref, through_ref,
):
    first = meta[SIDE] == 0
    own = dot(b_own[...], weighted_inputs(x_ref[...], step_ref[0], w_ref[0]), ((0,), (0,)))
    oth = dot(b_oth[...], sd_oth[0], ((0,), (0,)))
    d_own, d_oth = expand(end_ref[0]), expand(end_oth[0])
    one = jnp.ones_like(d_own)
    total = own * jnp.where(first, d_oth, one) + oth * jnp.where(first, one, d_own)
    total_ref[...] = total.astype(BF16)
    through_ref[...] = d_own * d_oth
    earlier = jnp.where(first, own, oth).astype(BF16)
    c_later = jnp.where(first, c_oth[...].astype(F32), c_own[...].astype(F32)).astype(BF16)
    inner_ref[...] = dot(c_later, earlier).astype(BF16)


def carried_body(hops, meta, *refs):
    recvs = refs[:hops]
    c_own, c_oth, inner_ref, end_ref, end_oth, own_ref, oth_ref = refs[hops:]
    first = meta[SIDE] == 0
    state = recvs[0][...]
    for r in recvs[1:]:
        state = state + r[...]
    d_own, d_oth = expand(end_ref[0]), expand(end_oth[0])
    one = jnp.ones_like(d_own)
    inner = inner_ref[...].astype(F32)
    zero = jnp.zeros_like(inner)
    own = dot(c_own[...], state) * jnp.where(first, one, d_oth) + jnp.where(first, zero, inner)
    oth = dot(c_oth[...], state) * jnp.where(first, d_own, one) + jnp.where(first, inner, zero)
    own_ref[...] = own.astype(BF16)
    oth_ref[...] = oth.astype(BF16)


def within_body(_, x_ref, step_ref, cum_ref, cumt_ref, skip_ref, b_ref, c_ref, out_ref):
    rows = x_ref.shape[0]
    above = lax.broadcasted_iota(jnp.int32, (rows, rows), 0) < lax.broadcasted_iota(
        jnp.int32, (rows, rows), 1
    )
    inter = jnp.where(above, 0.0, dot(c_ref[...], b_ref[...], ((1,), (1,))))
    lane = lax.broadcasted_iota(jnp.int32, (rows, 2 * WIDTH), 1)
    step, cum, skip = step_ref[0], cum_ref[0], skip_ref[0]
    for j in range(step.shape[1] // 2):
        cut = slice(j * 2 * WIDTH, (j + 1) * 2 * WIDTH)
        x = x_ref[:, cut].astype(F32)
        scaled = x * pair_columns(step, j)
        weights = []
        for h in (2 * j, 2 * j + 1):
            gap = jnp.minimum(cum[:, h : h + 1] - cumt_ref[0, h : h + 1, :], 0.0)
            weights.append((jnp.exp(gap) * inter).astype(BF16))
        stacked = jnp.concatenate(
            [
                jnp.where(lane < WIDTH, scaled, 0.0).astype(BF16),
                jnp.where(lane < WIDTH, 0.0, scaled).astype(BF16),
            ],
            axis=0,
        )
        out_ref[:, cut] = dot(jnp.concatenate(weights, axis=1), stacked) + x * pair_columns(skip, j)


def gate_body(pieces, meta, mixed_ref, gate_ref, cum_ref, gain_ref, *rest):
    out_ref = rest[-1]
    size = 2 * WIDTH

    def run(carried_ref):
        cum = jnp.exp(cum_ref[0])
        same = (
            lax.broadcasted_iota(jnp.int32, (size, size), 0) // WIDTH
            == lax.broadcasted_iota(jnp.int32, (size, size), 1) // WIDTH
        )
        mean = jnp.where(same, 1.0 / WIDTH, 0.0).astype(BF16)
        for j in range(cum.shape[1] // 2):
            cut = slice(j * size, (j + 1) * size)
            mixed = mixed_ref[:, cut] + carried_ref[:, cut].astype(F32) * pair_columns(cum, j)
            gate = gate_ref[:, cut].astype(F32)
            gated = mixed * (gate / (1.0 + jnp.exp(-gate)))
            square = gated * gated
            high = square.astype(BF16)
            low = (square - high.astype(F32)).astype(BF16)
            mean_square = dot(high, mean) + dot(low, mean)
            normed = gated * lax.rsqrt(mean_square + 1e-05) * gain_ref[:, cut]
            out_ref[:, cut] = normed.astype(BF16)

    for k in range(pieces):
        pl.when(pl.program_id(0) == k)(functools.partial(run, rest[k]))


def attend_body(per_used, planes, seg_len, order_at, meta, q_ref, *refs):
    keys, values = refs[0:2], refs[2:4]
    out_ref, bias = refs[4:]
    rows, total_rows = bias.shape
    per_block = rows // seg_len

    @pl.when(pl.program_id(0) == 0)
    def _():
        lane = lax.broadcasted_iota(jnp.int32, (1, total_rows), 1)
        row = lax.broadcasted_iota(jnp.int32, (rows, 1), 0)
        key_pos, query_pos = lane, row
        side, plane = meta[SIDE], meta[PLANE]
        at = 0
        for turned in (0, 1):
            for i in range(planes):
                block = 2 * (plane ^ i) + (side ^ turned)
                for k in range(per_block):
                    origin = meta[order_at + block * per_block + k] * seg_len
                    key_pos = jnp.where(
                        lane // seg_len == at, origin + lane - at * seg_len, key_pos
                    )
                    if turned == 0 and i == 0:
                        query_pos = jnp.where(
                            row // seg_len == k, origin + row - k * seg_len, query_pos
                        )
                    at += 1
        bias[...] = jnp.where(key_pos <= query_pos, 0.0, -jnp.inf)

    shape = (-1, ATT_DIM)
    key = jnp.concatenate([k[...].reshape(shape) for k in keys], axis=0)
    value = jnp.concatenate([v[...].reshape(shape) for v in values], axis=0)
    factor = ATT_DIM ** (-0.5) * math.log2(math.e)
    for r in range(per_used):
        cut = slice(r * ATT_DIM, (r + 1) * ATT_DIM)
        scores = dot(q_ref[:, cut], key, ((1,), (1,))) + bias[...]
        peak = jnp.max(scores, axis=1, keepdims=True)
        expos = jnp.exp2((scores - peak) * factor)
        total = jnp.sum(expos, axis=1, keepdims=True)
        out_ref[:, cut] = (dot(expos.astype(BF16), value) / total).astype(BF16)


def local(
    ssm_input, gate_input, step, log_decay, b_input, c_input, d_skip, norm_gain,
    queries, keys, values, segment_order,
):
    rows, heads = step.shape
    peers, here = lax.axis_size("seq"), lax.axis_index("seq")
    sub_index = lax.axis_index("sub")
    planes = peers // 2
    side, plane = here % 2, here // 2
    half = heads // 2
    count = CHUNKS
    per_chunk = half // count
    wide = per_chunk * WIDTH
    chunks = 2 * count
    swap = [(i, i ^ 1) for i in range(peers)]

    base = sub_index * heads
    group_of = lambda chunk: (base + chunk * per_chunk) // PER_GROUP
    order_at = GROUP + chunks
    meta = jnp.concatenate(
        [
            jnp.stack([side, side * count, (1 - side) * count, plane]),
            group_of(jnp.arange(chunks, dtype=jnp.int32)),
            segment_order,
        ]
    )

    stepb, cumb, wb, endb, cumt = call(
        scalars_body,
        (1,),
        [whole((rows, heads))] * 2,
        [whole((chunks, rows, per_chunk))] * 3 + [whole((chunks, 1, per_chunk)), whole((heads, rows))],
        [shaped((chunks, rows, per_chunk), F32)] * 3
        + [shaped((chunks, 1, per_chunk), F32), shaped((heads, rows), F32)],
    )(meta, step, log_decay)

    def narrow(origin, c=0, size=rows):
        return pl.BlockSpec((1, size, per_chunk), lambda i, m: (m[origin] + c + i, 0, 0))

    def columns(origin, c=0, size=rows):
        return pl.BlockSpec((size, wide), lambda i, m: (0, m[origin] + c + i))

    per_send = count // SENDS
    sd_oth = []
    for k in range(SENDS):
        at = k * per_send
        sd = call(
            send_body, (per_send,),
            [columns(GIVEN, at), narrow(GIVEN, at), narrow(GIVEN, at)],
            pl.BlockSpec((1, rows, wide), lambda i, m: (i, 0, 0)),
            shaped((per_send, rows, wide), BF16),
        )(meta, ssm_input, stepb, wb)
        sd_oth.append(lax.ppermute(sd, "seq", swap))

    groups_half = max(1, half // PER_GROUP)
    bc_start = ((base + (1 - side) * half) // PER_GROUP) * STATE
    bc_oth = lax.ppermute(
        jnp.concatenate(
            [
                lax.dynamic_slice_in_dim(b_input, bc_start, groups_half * STATE, 1),
                lax.dynamic_slice_in_dim(c_input, bc_start, groups_half * STATE, 1),
            ],
            axis=1,
        ),
        "seq",
        swap,
    )
    end_oth = lax.ppermute(
        lax.dynamic_slice_in_dim(endb, (1 - side) * count, count, 0), "seq", swap
    )

    query_count = queries.shape[1] // ATT_DIM
    ratio = ATT_HEADS // KV_HEADS
    used_heads = max(1, query_count // ratio)
    per_used = query_count // used_heads
    kv_wide = used_heads * ATT_DIM
    start = (sub_index * query_count // ratio) * ATT_DIM
    pack = jnp.concatenate(
        [
            lax.dynamic_slice_in_dim(keys, start, kv_wide, 1),
            lax.dynamic_slice_in_dim(values, start, kv_wide, 1),
        ],
        axis=1,
    )
    this_side = jnp.stack(
        [pack]
        + [
            lax.ppermute(pack, "seq", [(s, 2 * ((s // 2) ^ i) + s % 2) for s in range(peers)])
            for i in range(1, planes)
        ]
    )
    other_side = lax.ppermute(this_side, "seq", swap)

    def own_group(c):
        return pl.BlockSpec((rows, STATE), lambda i, m: (0, m[GROUP + m[OWN] + c]))

    def oth_group(c, at=0):
        at = at + c * per_chunk // PER_GROUP
        return pl.BlockSpec((rows, STATE), lambda i, m: (0, at))

    def oth_end(c):
        return pl.BlockSpec((1, 1, per_chunk), lambda i, m: (c, 0, 0))

    totals, inners, throughs = [], [], []
    for c in range(count):
        at = c % per_send
        total, inner, through = call(
            plane_body,
            (1,),
            [
                columns(OWN, c), narrow(OWN, c), narrow(OWN, c), narrow(OWN, c, 1),
                own_group(c), own_group(c),
                pl.BlockSpec((1, rows, wide), lambda i, m, at=at: (at, 0, 0)),
                oth_group(c), oth_group(c, groups_half), oth_end(c),
            ],
            [whole((STATE, wide)), whole((rows, wide)), whole((1, wide))],
            [shaped((STATE, wide), BF16), shaped((rows, wide), BF16), shaped((1, wide), F32)],
        )(
            meta, ssm_input, stepb, wb, endb, b_input, c_input,
            sd_oth[c // per_send], bc_oth, bc_oth, end_oth,
        )
        totals.append(total)
        inners.append(inner)
        throughs.append(through)

    sends = list(totals)
    received = [[] for _ in range(count)]
    for wave in range(count + planes - 2):
        for h in range(planes - 1):
            c = wave - h
            if not 0 <= c < count:
                continue
            got = lax.ppermute(sends[c], "seq", [(2 * h + x, 2 * h + 2 + x) for x in range(2)])
            received[c].append(got)
            if h < planes - 2:
                sends[c] = (throughs[c] * got.astype(F32) + totals[c].astype(F32)).astype(BF16)

    mixed = call(
        within_body,
        (chunks,),
        [
            pl.BlockSpec((rows, wide), lambda i, m: (0, i)),
            pl.BlockSpec((1, rows, per_chunk), lambda i, m: (i, 0, 0)),
            pl.BlockSpec((1, rows, per_chunk), lambda i, m: (i, 0, 0)),
            pl.BlockSpec((1, per_chunk, rows), lambda i, m: (i, 0, 0)),
            pl.BlockSpec((1, 1, per_chunk), lambda i, m: (i, 0, 0)),
            pl.BlockSpec((rows, STATE), lambda i, m: (0, m[GROUP + i])),
            pl.BlockSpec((rows, STATE), lambda i, m: (0, m[GROUP + i])),
        ],
        pl.BlockSpec((rows, wide), lambda i, m: (0, i)),
        shaped((rows, heads * WIDTH), F32),
    )(
        meta, ssm_input, stepb, cumb, cumt.reshape(chunks, per_chunk, rows),
        d_skip.reshape(chunks, 1, per_chunk), b_input, c_input,
    )

    gains = norm_gain.reshape(1, heads * WIDTH)

    def finish(mixer_out, origin, first, pieces):
        at = functools.partial(columns, origin, first)
        specs = [at(), at(), narrow(origin, first), at(1)]
        specs += [whole((rows, wide))] * len(pieces)
        args = [mixed, gate_input, cumb, gains, *pieces]
        aliases = {}
        if mixer_out is not None:
            specs.append(pl.BlockSpec(memory_space=pl.ANY))
            args.append(mixer_out)
            aliases = {len(args): 0}
        return call(
            functools.partial(gate_body, len(pieces)), (len(pieces),), specs, at(),
            shaped((rows, heads * WIDTH), BF16), aliases=aliases,
        )(meta, *args)

    owns, back = [], []
    for c in range(count):
        own, oth = call(
            functools.partial(carried_body, planes - 1),
            (1,),
            [whole((STATE, wide))] * (planes - 1)
            + [
                own_group(c), oth_group(c, groups_half), whole((rows, wide)),
                narrow(OWN, c, 1), oth_end(c),
            ],
            [whole((rows, wide))] * 2,
            [shaped((rows, wide), BF16)] * 2,
        )(meta, *received[c], c_input, bc_oth, inners[c], endb, end_oth)
        owns.append(own)
        back.append(lax.ppermute(oth, "seq", swap))
    mixer_out = finish(None, OWN, 0, owns)
    mixer_out = finish(mixer_out, GIVEN, 0, back[: count // 2])
    mixer_out = finish(mixer_out, GIVEN, count // 2, back[count // 2 :])

    seg_len = rows * peers // segment_order.shape[0]

    def kv_spec(at):
        return pl.BlockSpec((planes, rows, ATT_DIM), lambda g, m: (0, 0, at + g))

    head_block = pl.BlockSpec((rows, per_used * ATT_DIM), lambda g, m: (0, g))
    attn_out = call(
        functools.partial(attend_body, per_used, planes, seg_len, order_at),
        (used_heads,),
        [head_block, kv_spec(0), kv_spec(0), kv_spec(used_heads), kv_spec(used_heads)],
        head_block,
        shaped(queries.shape, BF16),
        scratch=[pltpu.VMEM((rows, rows * peers), F32)],
    )(meta, queries, this_side, other_side, this_side, other_side)
    return mixer_out, attn_out


def solution(mesh):
    tokens = ("groups", "seq")
    both = ("head", "sub")
    placed = (
        P(tokens, both), P(tokens, both), P(tokens, both), P(tokens, both),
        P(tokens, "head"), P(tokens, "head"), P(both), P(both),
        P(tokens, both), P(tokens, "head"), P(tokens, "head"), P("groups"),
    )
    return jax.shard_map(
        local,
        mesh=mesh,
        in_specs=placed,
        out_specs=(P(tokens, both), P(tokens, both)),
        check_vma=False,
    )
```
